32 devices in a mesh: row: 4 (over z), phi: 8 (over y, x, core).
Axes of the slice: x: 2, y: 2, z: 4, core: 2. Of those that a mesh axis runs over, the one named last changes fastest.
Arguments:
- fields: float32 [5, 64, 64, 4096], P(None, 'row', None, 'phi'), may hold values from -6 to 6
- offsets: int32 [64], P('row'), may hold values from 0 to 4095
- fraction: float32 [64], P('row'), may hold values from 0 to 1
- radial_diff: float32 [64], P('row'), may hold values from 0.05 to 0.15
- radial_drift: float32 [64], P('row'), may hold values from -0.05 to 0.05
- loop_diff: float32 [64], P('row'), may hold values from 0.05 to 0.15
- height_diff: float32 [64], replicated, may hold values from 0.05 to 0.15
Outputs:
- evolved: float32 [5, 64, 64, 4096], P(None, 'row', None, 'phi')
The draws below stay inside these ranges and needn't reach their ends.
All inputs are finite; a program needn't handle non-finite values.
Results may differ from the reference program's by a relative error of at most 0.00002.
Values sent between devices are 32-bit elements; how exact they have to be, the bound alone decides.
A program may use at most 128 MiB of HBM per device.

```python
import jax
import jax.numpy as jnp

FIELDS = 5
NZ = 64
NPHI = 4096
HYDRO = 2
NR = 64


def plant(array, own_key, low, high):
    place = [jax.random.randint(jax.random.fold_in(own_key, axis), (), 0, length) for axis, length in enumerate(array.shape)]
    longest = array.shape.index(max(array.shape))
    neighbour = place[:longest] + [(place[longest] + 1) % array.shape[longest]] + place[longest + 1:]
    return array.at[tuple(place)].set(low).at[tuple(neighbour)].set(high)


def level_of(own_key, shape, shards, smallest, largest):
    gain = 1.0
    for dim, parts in shards:
        draws = jax.random.uniform(jax.random.fold_in(jax.random.fold_in(own_key, 6), dim), (parts,), jnp.float32, smallest / len(shards), largest / len(shards))
        gain = gain * jnp.repeat(jnp.exp(draws), shape[dim] // parts).reshape((-1,) + (1,) * (len(shape) - 1 - dim))
    return gain


def normal_values(rng, shape, scale, limit, split=(), kind=jnp.bfloat16):
    values = jax.random.normal(rng, shape, jnp.float32) * scale
    if len(split) > 0:
        values = level_of(rng, shape, split, -0.22, 0.18) * values
    return jnp.clip(values, min=-limit, max=limit).astype(kind)


def setup_inputs(seed: int = 0) -> dict:
    streams_of = jax.random.split(jax.random.key(seed), 8)
    fields = normal_values(streams_of[0], (FIELDS, NR, NZ, NPHI), 1.0, 6.0, ((1, 4), (3, 8)), jnp.float32)
    offsets = plant(jax.random.randint(streams_of[1], (NR,), 0, NPHI), jax.random.fold_in(streams_of[1], 1), 0, NPHI - 1).astype(jnp.int32)
    fraction = jnp.clip(1.0 * jax.random.uniform(streams_of[2], (NR,), jnp.float32) ** level_of(streams_of[2], (NR,), ((0, 4),), -0.2, 0.2), 0.0, 1.0)
    radial_diff = jnp.clip(0.05 + 0.10000001 * jax.random.uniform(streams_of[3], (NR,), jnp.float32) ** level_of(streams_of[3], (NR,), ((0, 4),), -0.2, 0.2), 0.05, 0.15)
    radial_drift = jnp.clip(jax.random.uniform(streams_of[4], (NR,), jnp.float32, -0.05, 0.05) * level_of(streams_of[4], (NR,), ((0, 4),), -0.4, 0.0), -0.05, 0.05)
    loop_diff = jnp.clip(0.05 + 0.10000001 * jax.random.uniform(streams_of[5], (NR,), jnp.float32) ** level_of(streams_of[5], (NR,), ((0, 4),), -0.2, 0.2), 0.05, 0.15)
    height_diff = jnp.clip(jax.random.uniform(streams_of[6], (NZ,), jnp.float32, 0.05, 0.15), 0.05, 0.15)
    return dict(fields=fields, offsets=offsets, fraction=fraction, radial_diff=radial_diff, radial_drift=radial_drift, loop_diff=loop_diff, height_diff=height_diff)


def combine(state, upper, lower, east, west, above, below, radial_diff, radial_drift, loop_diff, height_diff):
    w_rad = radial_diff[None, :, None, None]
    v_rad = radial_drift[None, :, None, None]
    a_loop = loop_diff[None, :, None, None]
    c_height = height_diff[None, None, :, None]
    result = state + w_rad * (upper - 2.0 * state + lower) + v_rad * (upper - lower)
    result = result + a_loop * (east - 2.0 * state + west)
    return result + c_height * (above - 2.0 * state + below)


def reference(fields, offsets, fraction, radial_diff, radial_drift, loop_diff, height_diff):
    cells = jnp.arange(NPHI, dtype=jnp.int32)
    first_index = (cells[None, :] - offsets[:, None]) % NPHI
    second_index = (first_index - 1) % NPHI
    part_one = jnp.take_along_axis(fields, first_index[None, :, None, :], axis=3)
    part_two = jnp.take_along_axis(fields, second_index[None, :, None, :], axis=3)
    weight = fraction[None, :, None, None]
    state = (1.0 - weight) * part_one + weight * part_two
    for substep in range(HYDRO):
        radial_pad = jnp.pad(state, ((0, 0), (1, 1), (0, 0), (0, 0)))
        height_pad = jnp.pad(state, ((0, 0), (0, 0), (1, 1), (0, 0)))
        east = jnp.roll(state, -1, axis=3)
        west = jnp.roll(state, 1, axis=3)
        state = combine(state, radial_pad[:, 2:], radial_pad[:, :-2], east, west,
                        height_pad[:, :, 2:], height_pad[:, :, :-2],
                        radial_diff, radial_drift, loop_diff, height_diff)
    return state
```

```python
import functools

import jax
import jax.numpy as jnp
from jax import lax
from jax.experimental import pallas as pl
from jax.experimental.pallas import tpu as pltpu
from jax.sharding import PartitionSpec as P

LANES = 128
HALO = 2
MESH = pl.DeviceIdType.MESH


def kernel(
    n,
    rows,
    offs_in,
    frac_in,
    diff_in,
    drift_in,
    loop_in,
    rise_in,
    fields_ref,
    out_ref,
    *scratch,
):
    fields, radii, nz, width = fields_ref.shape
    per = radii // n
    half = n // 2
    tiles = width // LANES
    loop_tiles = tiles * n
    (
        loops,
        stage,
        pack,
        edge_stage,
        state,
        edges,
        extra,
        mid,
        coefs,
        height_ref,
        offs_ref,
        frac_ref,
        diff_ref,
        drift_ref,
        loop_ref,
        rise_ref,
        small_sem,
        in_send,
        in_recv,
        back_send,
        back_recv,
        edge_send,
        edge_recv,
        halo_send,
        halo_recv,
        coef_sem,
        own_sem,
    ) = scratch
    smalls = [
        pltpu.make_async_copy(source, target, small_sem.at[i])
        for i, (source, target) in enumerate(
            (
                (offs_in, offs_ref),
                (frac_in, frac_ref),
                (diff_in, diff_ref),
                (drift_in, drift_ref),
                (loop_in, loop_ref),
                (rise_in, rise_ref),
            )
        )
    ]
    for copy in smalls:
        copy.start()
    me = lax.axis_index("phi")
    row = lax.axis_index("row")
    has_low = row > 0
    has_high = row < rows - 1
    lane = lax.broadcasted_iota(jnp.int32, (nz, LANES), 1)
    zrow = lax.broadcasted_iota(jnp.int32, (nz, LANES), 0)

    barrier = pltpu.get_barrier_semaphore()
    for d in range(1, n):
        pl.semaphore_signal(
            barrier, inc=1, device_id={"phi": lax.rem(me + d, n)}, device_id_type=MESH
        )

    @pl.when(has_low)
    def _():
        pl.semaphore_signal(barrier, inc=1, device_id={"row": row - 1}, device_id_type=MESH)

    @pl.when(has_high)
    def _():
        pl.semaphore_signal(barrier, inc=1, device_id={"row": row + 1}, device_id_type=MESH)

    inner = jnp.logical_and(has_low, has_high)

    @pl.when(inner)
    def _():
        pl.semaphore_wait(barrier, n + 1)

    @pl.when(jnp.logical_not(inner))
    def _():
        pl.semaphore_wait(barrier, n)

    def radius(owner, ri):
        if ri == 1:
            return owner + half
        return jnp.where(owner < half, owner, owner + radii - n)

    def in_own(f, ri):
        return pltpu.make_async_copy(
            fields_ref.at[f, radius(me, ri)], loops.at[f, me, ri], own_sem.at[f, ri]
        )

    def in_copy(f, ri, d):
        to = lax.rem(me + d, n)
        return pltpu.make_async_remote_copy(
            src_ref=fields_ref.at[f, radius(to, ri)],
            dst_ref=loops.at[f, me, ri],
            send_sem=in_send.at[f, ri, d],
            recv_sem=in_recv.at[f, ri, d],
            device_id={"phi": to},
            device_id_type=MESH,
        )

    def back_copy(f, ri, d):
        to = lax.rem(me + d, n)
        return pltpu.make_async_remote_copy(
            src_ref=stage.at[f, to, ri],
            dst_ref=state.at[f, HALO + radius(me, ri)],
            send_sem=back_send.at[f, ri, d],
            recv_sem=back_recv.at[f, ri, d],
            device_id={"phi": to},
            device_id_type=MESH,
        )

    def edge_copy(f, d):
        to = lax.rem(me + d, n)
        return pltpu.make_async_remote_copy(
            src_ref=edge_stage.at[f, to],
            dst_ref=edges.at[f, me + HALO],
            send_sem=edge_send.at[f, d],
            recv_sem=edge_recv.at[f, d],
            device_id={"phi": to},
            device_id_type=MESH,
        )

    def back_own(f, ri):
        return pltpu.make_async_copy(
            stage.at[f, me, ri], state.at[f, HALO + radius(me, ri)], back_send.at[f, ri, 0]
        )

    def edge_own(f):
        return pltpu.make_async_copy(
            edge_stage.at[f, me], edges.at[f, me + HALO], edge_send.at[f, 0]
        )

    def halo_copies(f, low):
        side = 0 if low else 1
        source = HALO if low else radii
        target = radii + HALO if low else 0
        to = row - 1 if low else row + 1
        return (
            pltpu.make_async_remote_copy(
                src_ref=state.at[f, pl.ds(source, HALO)],
                dst_ref=state.at[f, pl.ds(target, HALO)],
                send_sem=halo_send.at[f, side, 0],
                recv_sem=halo_recv.at[f, side, 0],
                device_id={"row": to},
                device_id_type=MESH,
            ),
            pltpu.make_async_remote_copy(
                src_ref=edges.at[f, pl.ds(HALO if low else n, HALO)],
                dst_ref=edges.at[f, pl.ds(n + HALO if low else 0, HALO)],
                send_sem=halo_send.at[f, side, 1],
                recv_sem=halo_recv.at[f, side, 1],
                device_id={"row": to},
                device_id_type=MESH,
            ),
        )

    def coef_copy(low):
        side = 0 if low else 1
        return pltpu.make_async_remote_copy(
            src_ref=coefs.at[pl.ds(HALO if low else radii, HALO)],
            dst_ref=coefs.at[pl.ds(radii + HALO if low else 0, HALO)],
            send_sem=coef_sem.at[side],
            recv_sem=coef_sem.at[2 + side],
            device_id={"row": row - 1 if low else row + 1},
            device_id_type=MESH,
        )

    for f in range(fields):
        for ri in range(per):
            for d in range(1, n):
                in_copy(f, ri, d).start()
            in_own(f, ri).start()

    for copy in smalls:
        copy.wait()

    def fill_coefs(i, carry):
        diff = jnp.full((1, LANES), diff_ref[i], jnp.float32)
        drift = jnp.full((1, LANES), drift_ref[i], jnp.float32)
        loop = jnp.full((1, LANES), loop_ref[i], jnp.float32)
        coefs[HALO + i, 0:1, :] = diff + drift
        coefs[HALO + i, 1:2, :] = diff - drift
        coefs[HALO + i, 2:3, :] = loop
        coefs[HALO + i, 3:4, :] = 1.0 - 2.0 * (diff + loop)
        coefs[HALO + i, 4:5, :] = jnp.full((1, LANES), frac_ref[i], jnp.float32)
        coefs[HALO + i, 5:8, :] = jnp.zeros((3, LANES), jnp.float32)
        return carry

    lax.fori_loop(0, radii, fill_coefs, 0)

    def fill_height(z, carry):
        height_ref[pl.ds(z, 1), :] = jnp.full((1, LANES), rise_ref[z], jnp.float32)
        return carry

    lax.fori_loop(0, nz, fill_height, 0)

    @pl.when(has_low)
    def _():
        coef_copy(True).start()

    @pl.when(has_high)
    def _():
        coef_copy(False).start()


    @pl.when(jnp.logical_not(has_low))
    def _():
        state[:, 0:HALO] = jnp.zeros((fields, HALO, nz, width), jnp.float32)
        edges[:, 0:HALO] = jnp.zeros((fields, HALO) + edges.shape[2:], jnp.float32)
        coefs[0:HALO] = jnp.zeros((HALO,) + coefs.shape[1:], jnp.float32)

    @pl.when(jnp.logical_not(has_high))
    def _():
        state[:, radii + HALO :] = jnp.zeros((fields, HALO, nz, width), jnp.float32)
        edges[:, n + HALO :] = jnp.zeros((fields, HALO) + edges.shape[2:], jnp.float32)
        coefs[radii + HALO :] = jnp.zeros((HALO,) + coefs.shape[1:], jnp.float32)

    lane8 = lax.broadcasted_iota(jnp.int32, (8, LANES), 1)

    def shift_field(f, carry):
        for ri in range(per):
            in_own(f, ri).wait()
            for d in range(1, n):
                in_copy(f, ri, d).wait_recv()

        def shift_loop(ri, carry):
            mine = jnp.where(ri == 0, radius(me, 0), radius(me, 1))
            offset = jnp.full((8, LANES), offs_ref[mine], jnp.int32)
            weight = jnp.broadcast_to(coefs[HALO + mine, 4:5, :], (8, LANES))
            keep = 1.0 - weight
            fine = offset & (LANES - 1)

            def shift_rows(group, carry):
                z0 = pl.multiple_of(group * 8, 8)
                cells = [
                    loops[f, t // tiles, ri, pl.ds(z0, 8), (t % tiles) * LANES : (t % tiles + 1) * LANES]
                    for t in range(loop_tiles)
                ]
                step = 1
                while step < LANES:
                    taken = (offset & step) != 0
                    cells = [jnp.where(taken, pltpu.roll(c, step, 1), c) for c in cells]
                    step *= 2
                inside = lane8 < fine
                cells = [
                    jnp.where(inside, cells[t - 1], cells[t]) for t in range(loop_tiles)
                ]
                step = 1
                while step < loop_tiles:
                    taken = (offset & (step * LANES)) != 0
                    cells = [
                        jnp.where(taken, cells[t - step], cells[t]) for t in range(loop_tiles)
                    ]
                    step *= 2
                turned = [pltpu.roll(c, 1, 1) for c in cells]
                moved = [
                    keep * cells[t] + weight * jnp.where(lane8 == 0, turned[t - 1], turned[t])
                    for t in range(loop_tiles)
                ]
                for t in range(loop_tiles):
                    at = (t % tiles) * LANES
                    stage[f, t // tiles, ri, pl.ds(z0, 8), at : at + LANES] = moved[t]
                for q in range(n):
                    right = moved[(tiles * q + tiles) % loop_tiles]
                    both = jnp.where(lane8 < LANES // 2, right, moved[tiles * q - 1])
                    pack[ri, q, pl.ds(z0, 8), :] = both
                return carry

            return lax.fori_loop(0, nz // 8, shift_rows, carry)

        lax.fori_loop(0, per, shift_loop, 0)

        def pack_edges(q, carry):
            tile = pltpu.roll(pack[0, q], 2, 1)
            for ri in range(1, per):
                tile = jnp.where(lane < 4 * ri, tile, pltpu.roll(pack[ri, q], 2 + 4 * ri, 1))
            square = jnp.concatenate([tile] * (LANES // nz), axis=0).T
            edge_stage[f, q] = square[0 : 4 * per]
            return carry

        lax.fori_loop(0, n, pack_edges, 0)
        edge_own(f).start()
        for d in range(1, n):
            edge_copy(f, d).start()
        for ri in range(per):
            back_own(f, ri).start()
            for d in range(1, n):
                back_copy(f, ri, d).start()
        return carry

    lax.fori_loop(0, fields, shift_field, 0)

    @pl.when(has_low)
    def _():
        coef_copy(False).wait_recv()

    @pl.when(has_high)
    def _():
        coef_copy(True).wait_recv()

    def blend(cur, prev_tile, next_tile, up, low, where_r, height, height2):
        k_up = coefs[where_r, 0:1, :]
        k_low = coefs[where_r, 1:2, :]
        k_loop = coefs[where_r, 2:3, :]
        k_mid = coefs[where_r, 3:4, :]
        west = jnp.where(lane == 0, pltpu.roll(prev_tile, 1, 1), pltpu.roll(cur, 1, 1))
        east = jnp.where(
            lane == LANES - 1,
            pltpu.roll(next_tile, LANES - 1, 1),
            pltpu.roll(cur, LANES - 1, 1),
        )
        below = jnp.where(zrow == 0, 0.0, pltpu.roll(cur, 1, 0))
        above = jnp.where(zrow == nz - 1, 0.0, pltpu.roll(cur, nz - 1, 0))
        total = (k_mid - height2) * cur + k_up * up + k_low * low
        return total + k_loop * (east + west) + height * (above + below)

    for f in range(fields):
        edge_own(f).wait()
        back_own(f, 0).wait()
        for d in range(1, n):
            edge_copy(f, d).wait_recv()
            back_copy(f, 0, d).wait_recv()

        @pl.when(has_low)
        def _(f=f):
            for copy in halo_copies(f, True):
                copy.start()

        @pl.when(has_high)
        def _(f=f):
            for copy in halo_copies(f, False):
                copy.start()

        @pl.when(has_low)
        def _(f=f):
            for copy in halo_copies(f, False):
                copy.wait_recv()

        @pl.when(has_high)
        def _(f=f):
            for copy in halo_copies(f, True):
                copy.wait_recv()

        lines = edges[f].reshape((n + 2 * HALO) * 4 * per, LANES)
        square = jnp.concatenate([lines, lines[0 : LANES - lines.shape[0]]], axis=0).T[0:nz]
        for i in range(radii + 2 * HALO):
            r = i - HALO
            if r < half:
                at = 8 * i
            elif r < half + n:
                at = 8 * (HALO + r - half) + 4
            else:
                at = 8 * (HALO + r - radii + n)
            extra[i] = pltpu.roll(square, (2 * LANES - 2 - at) % LANES, 1)

        def first(i, carry, f=f):
            height = height_ref[...]
            height2 = height + height

            def tile(r, t):
                if t == tiles:
                    return extra[r]
                return state[f, r, :, pl.ds(t * LANES, LANES)]

            for t in range(tiles + 1):
                mid[i - 1, :, pl.ds(t * LANES, LANES)] = blend(
                    tile(i, t),
                    tile(i, (t + tiles) % (tiles + 1)),
                    tile(i, (t + 1) % (tiles + 1)),
                    tile(i + 1, t),
                    tile(i - 1, t),
                    i,
                    height,
                    height2,
                )
            return carry

        lax.fori_loop(1, half + 1, first, 0)
        lax.fori_loop(radii + 2 * HALO - 1 - half, radii + 2 * HALO - 1, first, 0)

        @pl.when(jnp.logical_not(has_low))
        def _():
            mid[0] = jnp.zeros(mid.shape[1:], jnp.float32)

        @pl.when(jnp.logical_not(has_high))
        def _():
            mid[radii + 1] = jnp.zeros(mid.shape[1:], jnp.float32)

        def second(i, carry, f=f):
            height = height_ref[...]
            height2 = height + height

            def tile(r, t):
                return mid[r, :, pl.ds(t * LANES, LANES)]

            for t in range(tiles):
                out_ref[f, i - 1, :, pl.ds(t * LANES, LANES)] = blend(
                    tile(i, t),
                    tile(i, (t + tiles) % (tiles + 1)),
                    tile(i, (t + 1) % (tiles + 1)),
                    tile(i + 1, t),
                    tile(i - 1, t),
                    i + 1,
                    height,
                    height2,
                )
            return carry

        lax.fori_loop(1, half - 1, second, 0)
        lax.fori_loop(radii - half + 3, radii + 1, second, 0)
        back_own(f, 1).wait()
        for d in range(1, n):
            back_copy(f, 1, d).wait_recv()
        lax.fori_loop(half + 1, radii + 2 * HALO - 1 - half, first, 0)
        lax.fori_loop(half - 1, radii - half + 3, second, 0)

    for f in range(fields):
        for d in range(1, n):
            edge_copy(f, d).wait_send()
            for ri in range(per):
                in_copy(f, ri, d).wait_send()
                back_copy(f, ri, d).wait_send()

        @pl.when(has_low)
        def _(f=f):
            for copy in halo_copies(f, True):
                copy.wait_send()

        @pl.when(has_high)
        def _(f=f):
            for copy in halo_copies(f, False):
                copy.wait_send()

    @pl.when(has_low)
    def _():
        coef_copy(True).wait_send()

    @pl.when(has_high)
    def _():
        coef_copy(False).wait_send()


def local(n, rows, fields, offsets, fraction, radial_diff, radial_drift, loop_diff, height_diff):
    count, radii, nz, width = fields.shape
    per = radii // n
    full = radii + 2 * HALO
    wide = width + LANES
    f32 = jnp.float32
    dma = pltpu.SemaphoreType.DMA
    scratch = [
        pltpu.VMEM((count, n, per, nz, width), f32),
        pltpu.VMEM((count, n, per, nz, width), f32),
        pltpu.VMEM((per, n, nz, LANES), f32),
        pltpu.VMEM((count, n, 4 * per, LANES), f32),
        pltpu.VMEM((count, full, nz, width), f32),
        pltpu.VMEM((count, n + 2 * HALO, 4 * per, LANES), f32),
        pltpu.VMEM((full, nz, LANES), f32),
        pltpu.VMEM((full - 2, nz, wide), f32),
        pltpu.VMEM((full, 8, LANES), f32),
        pltpu.VMEM((nz, LANES), f32),
        pltpu.SMEM((radii,), jnp.int32),
        pltpu.SMEM((radii,), f32),
        pltpu.SMEM((radii,), f32),
        pltpu.SMEM((radii,), f32),
        pltpu.SMEM((radii,), f32),
        pltpu.SMEM((nz,), f32),
        dma((6,)),
        dma((count, per, n)),
        dma((count, per, n)),
        dma((count, per, n)),
        dma((count, per, n)),
        dma((count, n)),
        dma((count, n)),
        dma((count, 2, 2)),
        dma((count, 2, 2)),
        dma((4,)),
        dma((count, per)),
    ]
    hbm = pl.BlockSpec(memory_space=pltpu.HBM)
    return pl.pallas_call(
        functools.partial(kernel, n, rows),
        out_shape=pltpu.VMEM(fields.shape, f32),
        in_specs=[hbm] * 7,
        out_specs=pl.BlockSpec(memory_space=pltpu.VMEM),
        scratch_shapes=scratch,
        compiler_params=pltpu.CompilerParams(
            collective_id=0, has_side_effects=True, vmem_limit_bytes=56557568
        ),
    )(offsets, fraction, radial_diff, radial_drift, loop_diff, height_diff, fields)


EARLY = 64
SINGLE = 64
LEVELS = (164, 176, 200)
ROUTED = 8


def ranges(sign, start, length, base, width, loop):
    delta = (sign + start - base) & (loop - 1)
    head = delta < width
    first = jnp.where(head, delta, 0)
    tail = jnp.clip(delta + length - loop, 0, width)
    return first, jnp.where(head, jnp.minimum(width - delta, length), tail)


def plan_kernel(rows, levels, offs_ref, load_ref, send_ref, level_ref, need_ref, got_ref, send_sem, recv_sem):
    radii = offs_ref.shape[0]
    wide = send_ref.shape[1]
    row = lax.axis_index("row")
    me = lax.axis_index("phi")
    barrier = pltpu.get_barrier_semaphore()
    for d in range(1, rows):
        pl.semaphore_signal(
            barrier, inc=1, device_id={"row": lax.rem(row + d, rows)}, device_id_type=MESH
        )
    x = lax.rem(me // 2, 2)
    y = me // 4
    tiles = 8
    loop = 32
    shape = (radii, wide)
    at = lax.broadcasted_iota(jnp.int32, shape, 0)
    k = lax.broadcasted_iota(jnp.int32, shape, 1)
    offset = jnp.zeros(shape, jnp.int32)
    for r in range(radii):
        offset = jnp.where(at == r, jnp.full(shape, offs_ref[r], jnp.int32), offset)
    window = (0 - offset) & (loop * LANES - 1)
    first = window >> 7
    fine = window & (LANES - 1)
    low = jnp.where(fine < 3, -1, 0)
    high = jnp.where(fine == LANES - 1, tiles + 1, tiles)
    length = high - low + 1
    start = first + low

    def before(count):
        total = count
        step = 1
        while step < radii:
            total = total + jnp.where(at >= step, pltpu.roll(total, step, 0), 0)
            step *= 2
        whole = jnp.broadcast_to(total[radii - 1 : radii], shape)
        return total - count, whole

    def piece(chip, base, width, size):
        return ranges(8 * chip, start, size, base, width, loop)

    def plan(ys, xs):
        chip = 2 * ys + xs
        other = 2 * (1 - ys) + xs
        p0 = piece(1 - xs, 8 * chip, tiles, length)
        p1 = piece(3 - xs, 8 * chip, tiles, length)
        target = 2 * ys + 1 - xs
        q0 = piece(target, 8 * chip, tiles, length)
        q1 = piece(target, 8 * other, tiles, length)
        u = piece(2 * (1 - ys), 8 * chip, tiles, length + tiles)
        v = piece(other, 16 * ys, 2 * tiles, length)
        p_at, p_all = before(p0[1] + p1[1])
        q_at, q_all = before(q0[1] + q1[1])
        u_at, u_all = before(u[1])
        v_at, v_all = before(v[1])
        q_at = q_at + jnp.maximum(p_all, EARLY)
        v_at = v_at + jnp.maximum(u_all, EARLY)
        need = jnp.maximum(jnp.maximum(p_all, EARLY) + q_all, jnp.maximum(u_all, EARLY) + v_all)
        need = jnp.maximum(need, jnp.maximum(p_all, u_all) + SINGLE)
        return p0, p1, p_at, q0, q1, q_at, u, u_at, v, v_at, need

    mine = plan(y, x)
    from_x = plan(y, 1 - x)
    from_y = plan(1 - y, x)

    need_ref[...] = jnp.maximum(mine[-1], from_x[-1])[0:8, 0:LANES].astype(jnp.float32)
    pl.semaphore_wait(barrier, rows - 1)
    copies = [
        pltpu.make_async_remote_copy(
            src_ref=need_ref,
            dst_ref=got_ref.at[d],
            send_sem=send_sem.at[d],
            recv_sem=recv_sem.at[d],
            device_id={"row": lax.rem(row + d, rows)},
            device_id_type=MESH,
        )
        for d in range(1, rows)
    ]
    for copy in copies:
        copy.start()

    def pick(rank, count, value, so_far):
        return jnp.where((rank >= 0) & (rank < count), value, so_far)

    none = jnp.zeros(shape, jnp.int32)
    p0, p1, p_at, q0, q1, q_at, u, u_at, v, v_at, _ = mine
    fx_p0, fx_p1, fx_p_at, fx_q0, fx_q1, fx_q_at = from_x[:6]
    fy_u, fy_u_at, fy_v, fy_v_at = from_y[6:10]
    rank = k - p_at
    out = pick(rank, p0[1], 16 * (p0[0] + rank) + at, none)
    rank = rank - p0[1]
    out = pick(rank, p1[1], 16 * (p1[0] + rank) + at, out)
    rank = k - q_at
    out = pick(rank, q0[1], 256 + 16 * (q0[0] + rank) + at, out)
    rank = rank - q0[1]
    out = pick(rank, q1[1], 512 + fy_u_at + q1[0] + rank - fy_u[0], out)
    send_ref[0:1] = jnp.sum(out, axis=0, keepdims=True)

    rank = k - u_at
    out = pick(rank, u[1], 16 * (u[0] + rank) + at, none)
    rank = k - v_at
    place = v[0] + rank
    near = place & (tiles - 1)
    second = jnp.where(y == 1, fx_p_at - fx_p0[0], fx_p_at + fx_p0[1] - fx_p1[0])
    value = jnp.where((place >> 3) == x, 256 + 16 * near + at, 512 + second + near)
    out = pick(rank, v[1], value, out)
    send_ref[1:2] = jnp.sum(out, axis=0, keepdims=True)
    send_ref[2:8] = jnp.zeros((6, wide), jnp.int32)

    chip = 2 * y + x
    i = (k & 15) - 1
    j = (8 * chip + first + i) & (loop - 1)
    owner = j >> 3
    near = j & (tiles - 1)
    own = 16 * near + at
    direct = jnp.where(y == 0, fx_p_at - fx_p0[0], fx_p_at + fx_p0[1] - fx_p1[0])
    alpha = jnp.where(
        owner == 2 * y + 1 - x,
        256 + direct + near,
        512 + fy_v_at + (j & 15) - fy_v[0],
    )
    beta = jnp.where(
        owner == 2 * (1 - y) + x,
        256 + fy_u_at + near - fy_u[0],
        jnp.where(
            owner == 2 * y + 1 - x,
            512 + fx_q_at + near - fx_q0[0],
            512 + fx_q_at + fx_q0[1] + near - fx_q1[0],
        ),
    )
    value = jnp.where(owner == chip, own, jnp.where(k < 16, alpha, beta))
    value = jnp.where((i >= low) & (i <= high), value, 0)
    value = jnp.where(k == 32, fine, value)
    load_ref[...] = value[:, 0:LANES]

    need = need_ref[...]
    for d in range(1, rows):
        copies[d - 1].wait_recv()
        need = jnp.maximum(need, got_ref[d])
    most = jnp.max(need)
    level = jnp.int32(0)
    for size in levels:
        level = level + jnp.where(most > size, 1, 0)
    level_ref[0] = level
    for copy in copies:
        copy.wait_send()


def routed_kernel(
    rows,
    slots,
    load_in,
    send_in,
    frac_in,
    diff_in,
    drift_in,
    loop_in,
    rise_in,
    fields_ref,
    out_ref,
    *scratch,
):
    fields, radii, nz, width = fields_ref.shape
    tiles = width // LANES
    pairs = 2 * fields
    deep = nz // 8
    group = 4
    single = slots - SINGLE
    scratch = list(scratch)

    def take(count):
        taken = scratch[:count]
        del scratch[:count]
        return taken

    own_a = take(pairs)
    own_b = take(pairs)
    got_x = take(pairs + 1)
    got_y = take(pairs + 1)
    out_x = take(2)
    out_y = take(2)
    stage = take(2)
    (
        state,
        mid,
        coefs,
        height_ref,
        load_ref,
        send_ref,
        frac_ref,
        diff_ref,
        drift_ref,
        loop_ref,
        rise_ref,
        small_sem,
        own_sem,
        pair_send,
        pair_recv,
        x_send,
        x_recv,
        y_send,
        y_recv,
        core_own,
        core_send,
        core_recv,
        halo_send,
        halo_recv,
        coef_sem,
    ) = scratch
    smalls = [
        pltpu.make_async_copy(source, target, small_sem.at[i])
        for i, (source, target) in enumerate(
            (
                (load_in, load_ref),
                (send_in, send_ref),
                (frac_in, frac_ref),
                (diff_in, diff_ref),
                (drift_in, drift_ref),
                (loop_in, loop_ref),
                (rise_in, rise_ref),
            )
        )
    ]
    for copy in smalls:
        copy.start()
    me = lax.axis_index("phi")
    row = lax.axis_index("row")
    core = lax.rem(me, 2)
    x = lax.rem(me // 2, 2)
    y = me // 4
    sibling = me + 1 - 2 * core
    x_peer = me + 2 - 4 * x
    y_peer = me + 4 - 8 * y
    has_low = row > 0
    has_high = row < rows - 1
    lane = lax.broadcasted_iota(jnp.int32, (nz, LANES), 1)
    zrow = lax.broadcasted_iota(jnp.int32, (nz, LANES), 0)
    lane8 = lax.broadcasted_iota(jnp.int32, (8, LANES), 1)

    def own_copies(n, there):
        result = []
        for part, owns in enumerate((own_a, own_b)):
            z0 = pl.multiple_of(
                (1 - core if there else core) * (nz // 2) + (n % 2) * 16 + part * 8, 8
            )
            for t in range(tiles):
                source = fields_ref.at[n // 2, :, pl.ds(z0, 8), pl.ds(t * LANES, LANES)]
                target = owns[n].at[pl.ds((tiles * core + t) * radii, radii)]
                i = part * tiles + t
                if there:
                    result.append(
                        pltpu.make_async_remote_copy(
                            src_ref=source,
                            dst_ref=target,
                            send_sem=pair_send.at[n, i],
                            recv_sem=pair_recv.at[n, i],
                            device_id={"phi": sibling},
                            device_id_type=MESH,
                        )
                    )
                else:
                    result.append(pltpu.make_async_copy(source, target, own_sem.at[n, i]))
        return result

    for n in range(pairs):
        for copy in own_copies(n, False):
            copy.start()

    barrier = pltpu.get_barrier_semaphore()
    for peer in (sibling, x_peer, y_peer):
        pl.semaphore_signal(barrier, inc=1, device_id={"phi": peer}, device_id_type=MESH)

    @pl.when(has_low)
    def _():
        pl.semaphore_signal(barrier, inc=1, device_id={"row": row - 1}, device_id_type=MESH)

    @pl.when(has_high)
    def _():
        pl.semaphore_signal(barrier, inc=1, device_id={"row": row + 1}, device_id_type=MESH)

    inner = jnp.logical_and(has_low, has_high)

    @pl.when(inner)
    def _():
        pl.semaphore_wait(barrier, 5)

    @pl.when(jnp.logical_not(inner))
    def _():
        pl.semaphore_wait(barrier, 4)

    for n in range(pairs):
        for copy in own_copies(n, True):
            copy.start()

    def parts(n):
        result = []
        if n < pairs:
            result.append((0, EARLY))
        result.append((EARLY, slots if n > 0 else single))
        return result

    def message(axis, n, which):
        begin, end = parts(n)[which]
        source, target = (out_x, got_x) if axis == 0 else (out_y, got_y)
        sends, recvs = (x_send, x_recv) if axis == 0 else (y_send, y_recv)
        return pltpu.make_async_remote_copy(
            src_ref=source[n % 2].at[pl.ds(begin, end - begin)],
            dst_ref=target[n].at[pl.ds(begin, end - begin)],
            send_sem=sends.at[n, which],
            recv_sem=recvs.at[n, which],
            device_id={"phi": x_peer if axis == 0 else y_peer},
            device_id_type=MESH,
        )

    def placed(n):
        z0 = pl.multiple_of(core * (nz // 2) + (n % 2) * 16, 8)
        return state.at[n // 2, pl.ds(HALO, radii), pl.ds(z0, 16)]

    def core_keep(n):
        return pltpu.make_async_copy(stage[n % 2].at[core], placed(n), core_own.at[n])

    def core_give(n):
        return pltpu.make_async_remote_copy(
            src_ref=stage[n % 2].at[1 - core],
            dst_ref=placed(n),
            send_sem=core_send.at[n],
            recv_sem=core_recv.at[n],
            device_id={"phi": sibling},
            device_id_type=MESH,
        )

    def halo_copy(f, low):
        side = 0 if low else 1
        source = HALO if low else radii
        target = radii + HALO if low else 0
        return pltpu.make_async_remote_copy(
            src_ref=state.at[f, pl.ds(source, HALO)],
            dst_ref=state.at[f, pl.ds(target, HALO)],
            send_sem=halo_send.at[f, side],
            recv_sem=halo_recv.at[f, side],
            device_id={"row": row - 1 if low else row + 1},
            device_id_type=MESH,
        )

    def coef_copy(low):
        side = 0 if low else 1
        return pltpu.make_async_remote_copy(
            src_ref=coefs.at[pl.ds(HALO if low else radii, HALO)],
            dst_ref=coefs.at[pl.ds(radii + HALO if low else 0, HALO)],
            send_sem=coef_sem.at[side],
            recv_sem=coef_sem.at[2 + side],
            device_id={"row": row - 1 if low else row + 1},
            device_id_type=MESH,
        )

    for copy in smalls:
        copy.wait()

    def choose(code, first, second, third, last, rest):
        a = first[jnp.minimum(code, 2 * tiles * radii - 1)]
        b = second[jnp.minimum(jnp.maximum(code - 256, 0), last)]
        c = third[jnp.maximum(code - 512, rest)]
        return jnp.where(code < 256, a, jnp.where(code < 512, b, c))

    def pack(axis, n, which):
        begin, end = parts(n)[which]
        target = (out_x if axis == 0 else out_y)[n % 2]
        fresh = (own_a if axis == 0 else own_b)[min(n, pairs - 1)]
        older = (own_b if axis == 0 else own_a)[max(n - 1, 0)]
        passed = (got_y if axis == 0 else got_x)[max(n - 1, 0)]
        only = n == 0 or end <= EARLY

        def step(i, carry):
            for lag in range(group):
                slot = begin + i * group + lag
                code = send_ref[axis, slot]
                if only:
                    target[slot] = fresh[jnp.minimum(code, 2 * tiles * radii - 1)]
                else:
                    target[slot] = choose(
                        code, fresh, older, passed, 2 * tiles * radii - 1, 0
                    )
            return carry

        lax.fori_loop(0, (end - begin) // group, step, 0)
        message(axis, n, which).start()

    def arrived(n):
        for copy in own_copies(n, False):
            copy.wait()
        for copy in own_copies(n, True):
            copy.wait_recv()

    def shift(n):
        target = stage[n % 2]

        def shift_radius(r, carry):
            fine = load_ref[r, 32]
            turn = (LANES - fine) & (LANES - 1)
            inside = lane8 < jnp.full((8, LANES), LANES - fine, jnp.int32)
            weight = jnp.broadcast_to(coefs[HALO + r, 4:5, :], (8, LANES))
            keep = 1.0 - weight
            for part in range(2):
                owns = (own_a if part == 0 else own_b)[n]
                near = (got_x if part == 0 else got_y)[n]
                far = (got_y if part == 0 else got_x)[n + 1]
                cells = []
                for i in range(2 * tiles + 3):
                    code = load_ref[r, 16 * part + i]
                    cells.append(
                        pltpu.roll(choose(code, owns, near, far, single - 1, EARLY), turn, 1)
                    )
                cells = [
                    jnp.where(inside, cells[i], cells[i + 1]) for i in range(2 * tiles + 2)
                ]
                turned = [pltpu.roll(c, 1, 1) for c in cells]
                moved = []
                for i in range(2 * tiles + 2):
                    before = turned[i]
                    if i > 0:
                        before = jnp.where(lane8 == 0, turned[i - 1], turned[i])
                    moved.append(keep * cells[i] + weight * before)
                z0 = 8 * part
                for half in range(2):
                    base = half * tiles
                    for t in range(tiles):
                        target[half, r, z0 : z0 + 8, t * LANES : (t + 1) * LANES] = moved[
                            base + t + 1
                        ]
                    target[half, r, z0 : z0 + 8, width : width + LANES] = jnp.where(
                        lane8 < LANES // 2, moved[base + tiles + 1], moved[base]
                    )
            return carry

        lax.fori_loop(0, radii, shift_radius, 0)
        core_keep(n).start()
        core_give(n).start()

    def blend(cur, prev_tile, next_tile, up, low, where_r, height, height2):
        k_up = coefs[where_r, 0:1, :]
        k_low = coefs[where_r, 1:2, :]
        k_loop = coefs[where_r, 2:3, :]
        k_mid = coefs[where_r, 3:4, :]
        west = jnp.where(lane == 0, pltpu.roll(prev_tile, 1, 1), pltpu.roll(cur, 1, 1))
        east = jnp.where(
            lane == LANES - 1,
            pltpu.roll(next_tile, LANES - 1, 1),
            pltpu.roll(cur, LANES - 1, 1),
        )
        below = jnp.where(zrow == 0, 0.0, pltpu.roll(cur, 1, 0))
        above = jnp.where(zrow == nz - 1, 0.0, pltpu.roll(cur, nz - 1, 0))
        total = (k_mid - height2) * cur + k_up * up + k_low * low
        return total + k_loop * (east + west) + height * (above + below)

    def first_substep(f, which):
        begin, end = ((1, radii + 3), (HALO + 1, radii + 1), (0, 2 * HALO))[which]

        def first(i, carry):
            if which == 2:
                i = jnp.where(i < HALO, i + 1, i + radii - 1)
            height = height_ref[...]
            height2 = height + height

            def tile(r, t):
                return state[f, r, :, pl.ds(t * LANES, LANES)]

            for t in range(tiles + 1):
                mid[i - 1, :, pl.ds(t * LANES, LANES)] = blend(
                    tile(i, t),
                    tile(i, (t + tiles) % (tiles + 1)),
                    tile(i, (t + 1) % (tiles + 1)),
                    tile(i + 1, t),
                    tile(i - 1, t),
                    i,
                    height,
                    height2,
                )
            return carry

        lax.fori_loop(begin, end, first, 0)

    def substeps(f):
        @pl.when(has_low)
        def _():
            halo_copy(f, False).wait_recv()

        @pl.when(has_high)
        def _():
            halo_copy(f, True).wait_recv()

        first_substep(f, 2 if f == fields - 1 else 0)

        @pl.when(jnp.logical_not(has_low))
        def _():
            mid[0] = jnp.zeros(mid.shape[1:], jnp.float32)

        @pl.when(jnp.logical_not(has_high))
        def _():
            mid[radii + 1] = jnp.zeros(mid.shape[1:], jnp.float32)

        def second(i, carry):
            height = height_ref[...]
            height2 = height + height

            def tile(r, t):
                return mid[r, :, pl.ds(t * LANES, LANES)]

            for t in range(tiles):
                out_ref[f, i - 1, :, pl.ds(t * LANES, LANES)] = blend(
                    tile(i, t),
                    tile(i, (t + tiles) % (tiles + 1)),
                    tile(i, (t + 1) % (tiles + 1)),
                    tile(i + 1, t),
                    tile(i - 1, t),
                    i + 1,
                    height,
                    height2,
                )
            return carry

        lax.fori_loop(1, radii + 1, second, 0)

    settled = set()

    def settle(n):
        if n not in settled:
            settled.add(n)
            core_keep(n).wait()

    arrived(0)
    for which in range(2):
        for axis in range(2):
            pack(axis, 0, which)

    def fill_coefs(i, carry):
        diff = jnp.full((1, LANES), diff_ref[i], jnp.float32)
        drift = jnp.full((1, LANES), drift_ref[i], jnp.float32)
        loop = jnp.full((1, LANES), loop_ref[i], jnp.float32)
        coefs[HALO + i, 0:1, :] = diff + drift
        coefs[HALO + i, 1:2, :] = diff - drift
        coefs[HALO + i, 2:3, :] = loop
        coefs[HALO + i, 3:4, :] = 1.0 - 2.0 * (diff + loop)
        coefs[HALO + i, 4:5, :] = jnp.full((1, LANES), frac_ref[i], jnp.float32)
        coefs[HALO + i, 5:8, :] = jnp.zeros((3, LANES), jnp.float32)
        return carry

    lax.fori_loop(0, radii, fill_coefs, 0)

    def fill_height(z, carry):
        height_ref[pl.ds(z, 1), :] = jnp.full((1, LANES), rise_ref[z], jnp.float32)
        return carry

    lax.fori_loop(0, nz, fill_height, 0)

    @pl.when(has_low)
    def _():
        coef_copy(True).start()

    @pl.when(has_high)
    def _():
        coef_copy(False).start()

    @pl.when(jnp.logical_not(has_low))
    def _():
        state[:, 0:HALO] = jnp.zeros((fields, HALO) + state.shape[2:], jnp.float32)
        coefs[0:HALO] = jnp.zeros((HALO,) + coefs.shape[1:], jnp.float32)

    @pl.when(jnp.logical_not(has_high))
    def _():
        state[:, radii + HALO :] = jnp.zeros((fields, HALO) + state.shape[2:], jnp.float32)
        coefs[radii + HALO :] = jnp.zeros((HALO,) + coefs.shape[1:], jnp.float32)

    arrived(1)
    for axis in range(2):
        pack(axis, 1, 0)

    @pl.when(has_low)
    def _():
        coef_copy(False).wait_recv()

    @pl.when(has_high)
    def _():
        coef_copy(True).wait_recv()

    for n in range(1, pairs + 3):
        if n <= pairs + 1:
            for axis in range(2):
                for which in range(len(parts(n - 1))):
                    message(axis, n - 1, which).wait_recv()
        if n <= pairs:
            last = len(parts(n)) - 1
            if n == pairs:
                for axis in range(2):
                    for which in range(2):
                        message(axis, n - 2, which).wait_send()
            for axis in range(2):
                pack(axis, n, last)
        if n + 1 < pairs:
            arrived(n + 1)
            for axis in range(2):
                for which in range(2):
                    message(axis, n - 1, which).wait_send()
                pack(axis, n + 1, 0)
        if 2 <= n <= pairs + 1:
            if n >= 4:
                settle(n - 4)
                core_give(n - 4).wait_send()
            shift(n - 2)
        f = (n - 4) // 2
        if n >= 4 and n % 2 == 0 and f < fields:
            for pair in (2 * f, 2 * f + 1):
                settle(pair)
                core_give(pair).wait_recv()

            @pl.when(has_low)
            def _(f=f):
                halo_copy(f, True).start()

            @pl.when(has_high)
            def _(f=f):
                halo_copy(f, False).start()

            if f == fields - 1:
                first_substep(f, 1)
            if n >= pairs:
                substeps(f)

        f = (n - 5) // 2
        if n >= 5 and n % 2 == 1 and n < pairs:
            substeps(f)

    for axis in range(2):
        for n in (pairs - 1, pairs):
            for which in range(len(parts(n))):
                message(axis, n, which).wait_send()
    for n in range(pairs):
        for copy in own_copies(n, True):
            copy.wait_send()
    for n in (pairs - 2, pairs - 1):
        core_give(n).wait_send()
    for f in range(fields):

        @pl.when(has_low)
        def _(f=f):
            halo_copy(f, True).wait_send()

        @pl.when(has_high)
        def _(f=f):
            halo_copy(f, False).wait_send()

    @pl.when(has_low)
    def _():
        coef_copy(True).wait_send()

    @pl.when(has_high)
    def _():
        coef_copy(False).wait_send()


def routed(rows, slots, which, load, send, fraction, radial_diff, radial_drift, loop_diff, height_diff, fields):
    count, radii, nz, width = fields.shape
    tiles = width // LANES
    pairs = 2 * count
    full = radii + 2 * HALO
    wide = width + LANES
    f32 = jnp.float32
    dma = pltpu.SemaphoreType.DMA
    scratch = [pltpu.VMEM((2 * tiles * radii, 8, LANES), f32)] * (2 * pairs)
    scratch += [pltpu.VMEM((slots, 8, LANES), f32)] * (2 * pairs + 2 + 4)
    scratch += [pltpu.VMEM((2, radii, 16, wide), f32)] * 2
    scratch += [
        pltpu.VMEM((count, full, nz, wide), f32),
        pltpu.VMEM((full - 2, nz, wide), f32),
        pltpu.VMEM((full, 8, LANES), f32),
        pltpu.VMEM((nz, LANES), f32),
        pltpu.SMEM(load.shape, jnp.int32),
        pltpu.SMEM(send.shape, jnp.int32),
        pltpu.SMEM((radii,), f32),
        pltpu.SMEM((radii,), f32),
        pltpu.SMEM((radii,), f32),
        pltpu.SMEM((radii,), f32),
        pltpu.SMEM((nz,), f32),
        dma((7,)),
        dma((pairs, 2 * tiles)),
        dma((pairs, 2 * tiles)),
        dma((pairs, 2 * tiles)),
        dma((pairs + 1, 2)),
        dma((pairs + 1, 2)),
        dma((pairs + 1, 2)),
        dma((pairs + 1, 2)),
        dma((pairs,)),
        dma((pairs,)),
        dma((pairs,)),
        dma((count, 2)),
        dma((count, 2)),
        dma((4,)),
    ]
    hbm = pl.BlockSpec(memory_space=pltpu.HBM)
    return pl.pallas_call(
        functools.partial(routed_kernel, rows, slots),
        out_shape=pltpu.VMEM(fields.shape, f32),
        in_specs=[hbm] * 8,
        out_specs=pl.BlockSpec(memory_space=pltpu.VMEM),
        scratch_shapes=scratch,
        compiler_params=pltpu.CompilerParams(
            collective_id=2 + which, has_side_effects=True, vmem_limit_bytes=56557568
        ),
    )(load, send, fraction, radial_diff, radial_drift, loop_diff, height_diff, fields)


def plan(rows, offsets):
    radii = offsets.shape[0]
    i32 = jnp.int32
    dma = pltpu.SemaphoreType.DMA
    vmem = pl.BlockSpec(memory_space=pltpu.VMEM)
    smem = pl.BlockSpec(memory_space=pltpu.SMEM)
    return pl.pallas_call(
        functools.partial(plan_kernel, rows, LEVELS),
        out_shape=(
            jax.ShapeDtypeStruct((radii, LANES), i32),
            jax.ShapeDtypeStruct((8, 2 * LANES), i32),
            jax.ShapeDtypeStruct((1,), i32),
        ),
        in_specs=[smem],
        out_specs=(vmem, vmem, smem),
        scratch_shapes=[
            pltpu.VMEM((8, LANES), jnp.float32),
            pltpu.VMEM((rows, 8, LANES), jnp.float32),
            dma((rows,)),
            dma((rows,)),
        ],
        compiler_params=pltpu.CompilerParams(collective_id=1, has_side_effects=True),
    )(offsets)


def adaptive(n, rows, fields, offsets, fraction, radial_diff, radial_drift, loop_diff, height_diff):
    if (n, fields.shape[1:]) != (ROUTED, (16, 64, 4 * LANES)):
        return local(
            n, rows, fields, offsets, fraction, radial_diff, radial_drift, loop_diff, height_diff
        )
    load, send, level = plan(rows, offsets)

    def through(which):
        return lambda load, send, offsets, *rest: routed(rows, LEVELS[which], which, load, send, *rest)

    def whole(load, send, offsets, fraction, radial_diff, radial_drift, loop_diff, height_diff, fields):
        return local(
            n, rows, fields, offsets, fraction, radial_diff, radial_drift, loop_diff, height_diff
        )

    branches = [through(which) for which in range(len(LEVELS))] + [whole]
    return lax.switch(
        level[0], branches, load, send, offsets, fraction, radial_diff, radial_drift, loop_diff,
        height_diff, fields,
    )


def solution(mesh):
    placed = (P(None, "row", None, "phi"), P("row"), P("row"), P("row"), P("row"), P("row"), P())
    body = functools.partial(adaptive, mesh.shape["phi"], mesh.shape["row"])
    return jax.shard_map(
        body, mesh=mesh, in_specs=placed, out_specs=P(None, "row", None, "phi"), check_vma=False
    )
```

```python
import functools

import jax
import jax.numpy as jnp
from jax import lax
from jax.experimental import pallas as pl
from jax.experimental.pallas import tpu as pltpu
from jax.sharding import PartitionSpec as P

LANES = 128
HALO = 2
MESH = pl.DeviceIdType.MESH


def kernel(
    n,
    rows,
    offs_in,
    frac_in,
    diff_in,
    drift_in,
    loop_in,
    rise_in,
    fields_ref,
    out_ref,
    *scratch,
):
    fields, radii, nz, width = fields_ref.shape
    per = radii // n
    half = n // 2
    tiles = width // LANES
    loop_tiles = tiles * n
    (
        loops,
        stage,
        pack,
        edge_stage,
        state,
        edges,
        extra,
        mid,
        coefs,
        height_ref,
        offs_ref,
        frac_ref,
        diff_ref,
        drift_ref,
        loop_ref,
        rise_ref,
        small_sem,
        in_send,
        in_recv,
        back_send,
        back_recv,
        edge_send,
        edge_recv,
        halo_send,
        halo_recv,
        coef_sem,
        own_sem,
    ) = scratch
    smalls = [
        pltpu.make_async_copy(source, target, small_sem.at[i])
        for i, (source, target) in enumerate(
            (
                (offs_in, offs_ref),
                (frac_in, frac_ref),
                (diff_in, diff_ref),
                (drift_in, drift_ref),
                (loop_in, loop_ref),
                (rise_in, rise_ref),
            )
        )
    ]
    for copy in smalls:
        copy.start()
    me = lax.axis_index("phi")
    row = lax.axis_index("row")
    has_low = row > 0
    has_high = row < rows - 1
    lane = lax.broadcasted_iota(jnp.int32, (nz, LANES), 1)
    zrow = lax.broadcasted_iota(jnp.int32, (nz, LANES), 0)

    barrier = pltpu.get_barrier_semaphore()
    for d in range(1, n):
        pl.semaphore_signal(
            barrier, inc=1, device_id={"phi": lax.rem(me + d, n)}, device_id_type=MESH
        )

    @pl.when(has_low)
    def _():
        pl.semaphore_signal(barrier, inc=1, device_id={"row": row - 1}, device_id_type=MESH)

    @pl.when(has_high)
    def _():
        pl.semaphore_signal(barrier, inc=1, device_id={"row": row + 1}, device_id_type=MESH)

    inner = jnp.logical_and(has_low, has_high)

    @pl.when(inner)
    def _():
        pl.semaphore_wait(barrier, n + 1)

    @pl.when(jnp.logical_not(inner))
    def _():
        pl.semaphore_wait(barrier, n)

    def radius(owner, ri):
        if ri == 1:
            return owner + half
        return jnp.where(owner < half, owner, owner + radii - n)

    def in_own(f, ri):
        return pltpu.make_async_copy(
            fields_ref.at[f, radius(me, ri)], loops.at[f, me, ri], own_sem.at[f, ri]
        )

    def in_copy(f, ri, d):
        to = lax.rem(me + d, n)
        return pltpu.make_async_remote_copy(
            src_ref=fields_ref.at[f, radius(to, ri)],
            dst_ref=loops.at[f, me, ri],
            send_sem=in_send.at[f, ri, d],
            recv_sem=in_recv.at[f, ri, d],
            device_id={"phi": to},
            device_id_type=MESH,
        )

    def back_copy(f, ri, d):
        to = lax.rem(me + d, n)
        return pltpu.make_async_remote_copy(
            src_ref=stage.at[f, to, ri],
            dst_ref=state.at[f, HALO + radius(me, ri)],
            send_sem=back_send.at[f, ri, d],
            recv_sem=back_recv.at[f, ri, d],
            device_id={"phi": to},
            device_id_type=MESH,
        )

    def edge_copy(f, d):
        to = lax.rem(me + d, n)
        return pltpu.make_async_remote_copy(
            src_ref=edge_stage.at[f, to],
            dst_ref=edges.at[f, me + HALO],
            send_sem=edge_send.at[f, d],
            recv_sem=edge_recv.at[f, d],
            device_id={"phi": to},
            device_id_type=MESH,
        )

    def back_own(f, ri):
        return pltpu.make_async_copy(
            stage.at[f, me, ri], state.at[f, HALO + radius(me, ri)], back_send.at[f, ri, 0]
        )

    def edge_own(f):
        return pltpu.make_async_copy(
            edge_stage.at[f, me], edges.at[f, me + HALO], edge_send.at[f, 0]
        )

    def halo_copies(f, low):
        side = 0 if low else 1
        source = HALO if low else radii
        target = radii + HALO if low else 0
        to = row - 1 if low else row + 1
        return (
            pltpu.make_async_remote_copy(
                src_ref=state.at[f, pl.ds(source, HALO)],
                dst_ref=state.at[f, pl.ds(target, HALO)],
                send_sem=halo_send.at[f, side, 0],
                recv_sem=halo_recv.at[f, side, 0],
                device_id={"row": to},
                device_id_type=MESH,
            ),
            pltpu.make_async_remote_copy(
                src_ref=edges.at[f, pl.ds(HALO if low else n, HALO)],
                dst_ref=edges.at[f, pl.ds(n + HALO if low else 0, HALO)],
                send_sem=halo_send.at[f, side, 1],
                recv_sem=halo_recv.at[f, side, 1],
                device_id={"row": to},
                device_id_type=MESH,
            ),
        )

    def coef_copy(low):
        side = 0 if low else 1
        return pltpu.make_async_remote_copy(
            src_ref=coefs.at[pl.ds(HALO if low else radii, HALO)],
            dst_ref=coefs.at[pl.ds(radii + HALO if low else 0, HALO)],
            send_sem=coef_sem.at[side],
            recv_sem=coef_sem.at[2 + side],
            device_id={"row": row - 1 if low else row + 1},
            device_id_type=MESH,
        )

    for f in range(fields):
        for ri in range(per):
            for d in range(1, n):
                in_copy(f, ri, d).start()
            in_own(f, ri).start()

    for copy in smalls:
        copy.wait()

    def fill_coefs(i, carry):
        diff = jnp.full((1, LANES), diff_ref[i], jnp.float32)
        drift = jnp.full((1, LANES), drift_ref[i], jnp.float32)
        loop = jnp.full((1, LANES), loop_ref[i], jnp.float32)
        coefs[HALO + i, 0:1, :] = diff + drift
        coefs[HALO + i, 1:2, :] = diff - drift
        coefs[HALO + i, 2:3, :] = loop
        coefs[HALO + i, 3:4, :] = 1.0 - 2.0 * (diff + loop)
        coefs[HALO + i, 4:5, :] = jnp.full((1, LANES), frac_ref[i], jnp.float32)
        coefs[HALO + i, 5:8, :] = jnp.zeros((3, LANES), jnp.float32)
        return carry

    lax.fori_loop(0, radii, fill_coefs, 0)

    def fill_height(z, carry):
        height_ref[pl.ds(z, 1), :] = jnp.full((1, LANES), rise_ref[z], jnp.float32)
        return carry

    lax.fori_loop(0, nz, fill_height, 0)

    @pl.when(has_low)
    def _():
        coef_copy(True).start()

    @pl.when(has_high)
    def _():
        coef_copy(False).start()


    @pl.when(jnp.logical_not(has_low))
    def _():
        state[:, 0:HALO] = jnp.zeros((fields, HALO, nz, width), jnp.float32)
        edges[:, 0:HALO] = jnp.zeros((fields, HALO) + edges.shape[2:], jnp.float32)
        coefs[0:HALO] = jnp.zeros((HALO,) + coefs.shape[1:], jnp.float32)

    @pl.when(jnp.logical_not(has_high))
    def _():
        state[:, radii + HALO :] = jnp.zeros((fields, HALO, nz, width), jnp.float32)
        edges[:, n + HALO :] = jnp.zeros((fields, HALO) + edges.shape[2:], jnp.float32)
        coefs[radii + HALO :] = jnp.zeros((HALO,) + coefs.shape[1:], jnp.float32)

    lane8 = lax.broadcasted_iota(jnp.int32, (8, LANES), 1)

    def shift_field(f, carry):
        for ri in range(per):
            in_own(f, ri).wait()
            for d in range(1, n):
                in_copy(f, ri, d).wait_recv()

        def shift_loop(ri, carry):
            mine = jnp.where(ri == 0, radius(me, 0), radius(me, 1))
            offset = jnp.full((8, LANES), offs_ref[mine], jnp.int32)
            weight = jnp.broadcast_to(coefs[HALO + mine, 4:5, :], (8, LANES))
            keep = 1.0 - weight
            fine = offset & (LANES - 1)

            def shift_rows(group, carry):
                z0 = pl.multiple_of(group * 8, 8)
                cells = [
                    loops[f, t // tiles, ri, pl.ds(z0, 8), (t % tiles) * LANES : (t % tiles + 1) * LANES]
                    for t in range(loop_tiles)
                ]
                step = 1
                while step < LANES:
                    taken = (offset & step) != 0
                    cells = [jnp.where(taken, pltpu.roll(c, step, 1), c) for c in cells]
                    step *= 2
                inside = lane8 < fine
                cells = [
                    jnp.where(inside, cells[t - 1], cells[t]) for t in range(loop_tiles)
                ]
                step = 1
                while step < loop_tiles:
                    taken = (offset & (step * LANES)) != 0
                    cells = [
                        jnp.where(taken, cells[t - step], cells[t]) for t in range(loop_tiles)
                    ]
                    step *= 2
                turned = [pltpu.roll(c, 1, 1) for c in cells]
                moved = [
                    keep * cells[t] + weight * jnp.where(lane8 == 0, turned[t - 1], turned[t])
                    for t in range(loop_tiles)
                ]
                for t in range(loop_tiles):
                    at = (t % tiles) * LANES
                    stage[f, t // tiles, ri, pl.ds(z0, 8), at : at + LANES] = moved[t]
                for q in range(n):
                    right = moved[(tiles * q + tiles) % loop_tiles]
                    both = jnp.where(lane8 < LANES // 2, right, moved[tiles * q - 1])
                    pack[ri, q, pl.ds(z0, 8), :] = both
                return carry

            return lax.fori_loop(0, nz // 8, shift_rows, carry)

        lax.fori_loop(0, per, shift_loop, 0)

        def pack_edges(q, carry):
            tile = pltpu.roll(pack[0, q], 2, 1)
            for ri in range(1, per):
                tile = jnp.where(lane < 4 * ri, tile, pltpu.roll(pack[ri, q], 2 + 4 * ri, 1))
            square = jnp.concatenate([tile] * (LANES // nz), axis=0).T
            edge_stage[f, q] = square[0 : 4 * per]
            return carry

        lax.fori_loop(0, n, pack_edges, 0)
        edge_own(f).start()
        for d in range(1, n):
            edge_copy(f, d).start()
        for ri in range(per):
            back_own(f, ri).start()
            for d in range(1, n):
                back_copy(f, ri, d).start()
        return carry

    lax.fori_loop(0, fields, shift_field, 0)

    @pl.when(has_low)
    def _():
        coef_copy(False).wait_recv()

    @pl.when(has_high)
    def _():
        coef_copy(True).wait_recv()

    def blend(cur, prev_tile, next_tile, up, low, where_r, height, height2):
        k_up = coefs[where_r, 0:1, :]
        k_low = coefs[where_r, 1:2, :]
        k_loop = coefs[where_r, 2:3, :]
        k_mid = coefs[where_r, 3:4, :]
        west = jnp.where(lane == 0, pltpu.roll(prev_tile, 1, 1), pltpu.roll(cur, 1, 1))
        east = jnp.where(
            lane == LANES - 1,
            pltpu.roll(next_tile, LANES - 1, 1),
            pltpu.roll(cur, LANES - 1, 1),
        )
        below = jnp.where(zrow == 0, 0.0, pltpu.roll(cur, 1, 0))
        above = jnp.where(zrow == nz - 1, 0.0, pltpu.roll(cur, nz - 1, 0))
        total = (k_mid - height2) * cur + k_up * up + k_low * low
        return total + k_loop * (east + west) + height * (above + below)

    def finish_field(f, carry):
        edge_own(f).wait()
        back_own(f, 0).wait()
        for d in range(1, n):
            edge_copy(f, d).wait_recv()
            back_copy(f, 0, d).wait_recv()

        @pl.when(has_low)
        def _(f=f):
            for copy in halo_copies(f, True):
                copy.start()

        @pl.when(has_high)
        def _(f=f):
            for copy in halo_copies(f, False):
                copy.start()

        @pl.when(has_low)
        def _(f=f):
            for copy in halo_copies(f, False):
                copy.wait_recv()

        @pl.when(has_high)
        def _(f=f):
            for copy in halo_copies(f, True):
                copy.wait_recv()

        lines = edges[f].reshape((n + 2 * HALO) * 4 * per, LANES)
        square = jnp.concatenate([lines, lines[0 : LANES - lines.shape[0]]], axis=0).T[0:nz]
        for i in range(radii + 2 * HALO):
            r = i - HALO
            if r < half:
                at = 8 * i
            elif r < half + n:
                at = 8 * (HALO + r - half) + 4
            else:
                at = 8 * (HALO + r - radii + n)
            extra[i] = pltpu.roll(square, (2 * LANES - 2 - at) % LANES, 1)

        def first(i, carry, f=f):
            height = height_ref[...]
            height2 = height + height

            def tile(r, t):
                if t == tiles:
                    return extra[r]
                return state[f, r, :, pl.ds(t * LANES, LANES)]

            for t in range(tiles + 1):
                mid[i - 1, :, pl.ds(t * LANES, LANES)] = blend(
                    tile(i, t),
                    tile(i, (t + tiles) % (tiles + 1)),
                    tile(i, (t + 1) % (tiles + 1)),
                    tile(i + 1, t),
                    tile(i - 1, t),
                    i,
                    height,
                    height2,
                )
            return carry

        lax.fori_loop(1, half + 1, first, 0)
        lax.fori_loop(radii + 2 * HALO - 1 - half, radii + 2 * HALO - 1, first, 0)

        @pl.when(jnp.logical_not(has_low))
        def _():
            mid[0] = jnp.zeros(mid.shape[1:], jnp.float32)

        @pl.when(jnp.logical_not(has_high))
        def _():
            mid[radii + 1] = jnp.zeros(mid.shape[1:], jnp.float32)

        def second(i, carry, f=f):
            height = height_ref[...]
            height2 = height + height

            def tile(r, t):
                return mid[r, :, pl.ds(t * LANES, LANES)]

            for t in range(tiles):
                out_ref[f, i - 1, :, pl.ds(t * LANES, LANES)] = blend(
                    tile(i, t),
                    tile(i, (t + tiles) % (tiles + 1)),
                    tile(i, (t + 1) % (tiles + 1)),
                    tile(i + 1, t),
                    tile(i - 1, t),
                    i + 1,
                    height,
                    height2,
                )
            return carry

        lax.fori_loop(1, half - 1, second, 0)
        lax.fori_loop(radii - half + 3, radii + 1, second, 0)
        back_own(f, 1).wait()
        for d in range(1, n):
            back_copy(f, 1, d).wait_recv()
        lax.fori_loop(half + 1, radii + 2 * HALO - 1 - half, first, 0)
        lax.fori_loop(half - 1, radii - half + 3, second, 0)
        return carry

    lax.fori_loop(0, fields, finish_field, 0)

    for f in range(fields):
        for d in range(1, n):
            edge_copy(f, d).wait_send()
            for ri in range(per):
                in_copy(f, ri, d).wait_send()
                back_copy(f, ri, d).wait_send()

        @pl.when(has_low)
        def _(f=f):
            for copy in halo_copies(f, True):
                copy.wait_send()

        @pl.when(has_high)
        def _(f=f):
            for copy in halo_copies(f, False):
                copy.wait_send()

    @pl.when(has_low)
    def _():
        coef_copy(True).wait_send()

    @pl.when(has_high)
    def _():
        coef_copy(False).wait_send()


def local(n, rows, fields, offsets, fraction, radial_diff, radial_drift, loop_diff, height_diff):
    count, radii, nz, width = fields.shape
    per = radii // n
    full = radii + 2 * HALO
    wide = width + LANES
    f32 = jnp.float32
    dma = pltpu.SemaphoreType.DMA
    scratch = [
        pltpu.VMEM((count, n, per, nz, width), f32),
        pltpu.VMEM((count, n, per, nz, width), f32),
        pltpu.VMEM((per, n, nz, LANES), f32),
        pltpu.VMEM((count, n, 4 * per, LANES), f32),
        pltpu.VMEM((count, full, nz, width), f32),
        pltpu.VMEM((count, n + 2 * HALO, 4 * per, LANES), f32),
        pltpu.VMEM((full, nz, LANES), f32),
        pltpu.VMEM((full - 2, nz, wide), f32),
        pltpu.VMEM((full, 8, LANES), f32),
        pltpu.VMEM((nz, LANES), f32),
        pltpu.SMEM((radii,), jnp.int32),
        pltpu.SMEM((radii,), f32),
        pltpu.SMEM((radii,), f32),
        pltpu.SMEM((radii,), f32),
        pltpu.SMEM((radii,), f32),
        pltpu.SMEM((nz,), f32),
        dma((6,)),
        dma((count, per, n)),
        dma((count, per, n)),
        dma((count, per, n)),
        dma((count, per, n)),
        dma((count, n)),
        dma((count, n)),
        dma((count, 2, 2)),
        dma((count, 2, 2)),
        dma((4,)),
        dma((count, per)),
    ]
    hbm = pl.BlockSpec(memory_space=pltpu.HBM)
    return pl.pallas_call(
        functools.partial(kernel, n, rows),
        out_shape=pltpu.VMEM(fields.shape, f32),
        in_specs=[hbm] * 7,
        out_specs=pl.BlockSpec(memory_space=pltpu.VMEM),
        scratch_shapes=scratch,
        compiler_params=pltpu.CompilerParams(
            collective_id=0, has_side_effects=True, vmem_limit_bytes=56557568
        ),
    )(offsets, fraction, radial_diff, radial_drift, loop_diff, height_diff, fields)


EARLY = 64
SINGLE = 64
LEVELS = (164, 172, 180, 196)
ROUTED = 8


def ranges(sign, start, length, base, width, loop):
    delta = (sign + start - base) & (loop - 1)
    head = delta < width
    first = jnp.where(head, delta, 0)
    tail = jnp.clip(delta + length - loop, 0, width)
    return first, jnp.where(head, jnp.minimum(width - delta, length), tail)


def plan_kernel(rows, levels, offs_ref, load_ref, send_ref, level_ref, need_ref, got_ref, send_sem, recv_sem):
    radii = offs_ref.shape[0]
    row = lax.axis_index("row")
    me = lax.axis_index("phi")
    barrier = pltpu.get_barrier_semaphore()
    for d in range(1, rows):
        pl.semaphore_signal(
            barrier, inc=1, device_id={"row": lax.rem(row + d, rows)}, device_id_type=MESH
        )
    x = lax.rem(me // 2, 2)
    y = me // 4
    tiles = 8
    loop = 32
    shape = (radii, LANES)
    at = lax.broadcasted_iota(jnp.int32, shape, 0)
    k = lax.broadcasted_iota(jnp.int32, shape, 1)
    offset = jnp.zeros(shape, jnp.int32)
    for r in range(radii):
        offset = jnp.where(at == r, jnp.full(shape, offs_ref[r], jnp.int32), offset)
    window = (0 - offset) & (loop * LANES - 1)
    first = window >> 7
    fine = window & (LANES - 1)
    low = jnp.where(fine < 3, -1, 0)
    high = jnp.where(fine == LANES - 1, tiles + 1, tiles)
    length = high - low + 1
    start = first + low

    def before(count):
        total = count
        step = 1
        while step < radii:
            total = total + jnp.where(at >= step, pltpu.roll(total, step, 0), 0)
            step *= 2
        whole = jnp.broadcast_to(total[radii - 1 : radii], shape)
        return total - count, whole

    def piece(chip, base, width, size):
        return ranges(8 * chip, start, size, base, width, loop)

    def plan(ys, xs):
        chip = 2 * ys + xs
        other = 2 * (1 - ys) + xs
        p0 = piece(1 - xs, 8 * chip, tiles, length)
        p1 = piece(3 - xs, 8 * chip, tiles, length)
        target = 2 * ys + 1 - xs
        q0 = piece(target, 8 * chip, tiles, length)
        q1 = piece(target, 8 * other, tiles, length)
        u = piece(2 * (1 - ys), 8 * chip, tiles, length + tiles)
        v = piece(other, 16 * ys, 2 * tiles, length)
        p_at, p_all = before(p0[1] + p1[1])
        q_at, q_all = before(q0[1] + q1[1])
        u_at, u_all = before(u[1])
        v_at, v_all = before(v[1])
        q_at = q_at + jnp.maximum(p_all, EARLY)
        v_at = v_at + jnp.maximum(u_all, EARLY)
        need = jnp.maximum(jnp.maximum(p_all, EARLY) + q_all, jnp.maximum(u_all, EARLY) + v_all)
        need = jnp.maximum(need, jnp.maximum(p_all, u_all) + SINGLE)
        return p0, p1, p_at, q0, q1, q_at, u, u_at, v, v_at, need

    mine = plan(y, x)
    from_x = plan(y, 1 - x)

    need_ref[...] = jnp.maximum(mine[-1], from_x[-1])[0:8].astype(jnp.float32)
    pl.semaphore_wait(barrier, rows - 1)
    copies = [
        pltpu.make_async_remote_copy(
            src_ref=need_ref,
            dst_ref=got_ref.at[d],
            send_sem=send_sem.at[d],
            recv_sem=recv_sem.at[d],
            device_id={"row": lax.rem(row + d, rows)},
            device_id_type=MESH,
        )
        for d in range(1, rows)
    ]
    for copy in copies:
        copy.start()

    from_y = plan(1 - y, x)

    def pick(rank, count, value, so_far):
        return jnp.where((rank >= 0) & (rank < count), value, so_far)

    none = jnp.zeros(shape, jnp.int32)
    p0, p1, p_at, q0, q1, q_at, u, u_at, v, v_at, _ = mine
    fx_p0, fx_p1, fx_p_at, fx_q0, fx_q1, fx_q_at = from_x[:6]
    fy_u, fy_u_at, fy_v, fy_v_at = from_y[6:10]
    for part in range(send_ref.shape[1] // LANES):
        slot = k + part * LANES
        columns = slice(part * LANES, (part + 1) * LANES)
        rank = slot - p_at
        out = pick(rank, p0[1], 16 * (p0[0] + rank) + at, none)
        rank = rank - p0[1]
        out = pick(rank, p1[1], 16 * (p1[0] + rank) + at, out)
        rank = slot - q_at
        out = pick(rank, q0[1], 256 + 16 * (q0[0] + rank) + at, out)
        rank = rank - q0[1]
        out = pick(rank, q1[1], 512 + fy_u_at + q1[0] + rank - fy_u[0], out)
        send_ref[0:1, columns] = jnp.sum(out, axis=0, keepdims=True)

        rank = slot - u_at
        out = pick(rank, u[1], 16 * (u[0] + rank) + at, none)
        rank = slot - v_at
        place = v[0] + rank
        near = place & (tiles - 1)
        second = jnp.where(y == 1, fx_p_at - fx_p0[0], fx_p_at + fx_p0[1] - fx_p1[0])
        value = jnp.where((place >> 3) == x, 256 + 16 * near + at, 512 + second + near)
        out = pick(rank, v[1], value, out)
        send_ref[1:2, columns] = jnp.sum(out, axis=0, keepdims=True)
    send_ref[2:8] = jnp.zeros((6, send_ref.shape[1]), jnp.int32)

    chip = 2 * y + x
    i = (k & 15) - 1
    j = (8 * chip + first + i) & (loop - 1)
    owner = j >> 3
    near = j & (tiles - 1)
    own = 16 * near + at
    direct = jnp.where(y == 0, fx_p_at - fx_p0[0], fx_p_at + fx_p0[1] - fx_p1[0])
    alpha = jnp.where(
        owner == 2 * y + 1 - x,
        256 + direct + near,
        512 + fy_v_at + (j & 15) - fy_v[0],
    )
    beta = jnp.where(
        owner == 2 * (1 - y) + x,
        256 + fy_u_at + near - fy_u[0],
        jnp.where(
            owner == 2 * y + 1 - x,
            512 + fx_q_at + near - fx_q0[0],
            512 + fx_q_at + fx_q0[1] + near - fx_q1[0],
        ),
    )
    value = jnp.where(owner == chip, own, jnp.where(k < 16, alpha, beta))
    value = jnp.where((i >= low) & (i <= high), value, 0)
    value = jnp.where(k == 32, fine, value)
    load_ref[...] = value

    need = need_ref[...]
    for d in range(1, rows):
        copies[d - 1].wait_recv()
        need = jnp.maximum(need, got_ref[d])
    most = jnp.max(need)
    level = jnp.int32(0)
    for size in levels:
        level = level + jnp.where(most > size, 1, 0)
    level_ref[0] = level
    for copy in copies:
        copy.wait_send()


def routed_kernel(
    rows,
    slots,
    load_in,
    send_in,
    frac_in,
    diff_in,
    drift_in,
    loop_in,
    rise_in,
    fields_ref,
    out_ref,
    *scratch,
):
    fields, radii, nz, width = fields_ref.shape
    tiles = width // LANES
    pairs = 2 * fields
    deep = nz // 8
    group = 4
    single = slots - SINGLE
    scratch = list(scratch)

    def take(count):
        taken = scratch[:count]
        del scratch[:count]
        return taken

    own_a = take(pairs)
    own_b = take(pairs)
    got_x = take(pairs + 1)
    got_y = take(pairs + 1)
    out_x = take(2)
    out_y = take(2)
    stage = take(2)
    (
        state,
        mid,
        coefs,
        height_ref,
        load_ref,
        send_ref,
        frac_ref,
        diff_ref,
        drift_ref,
        loop_ref,
        rise_ref,
        small_sem,
        own_sem,
        pair_send,
        pair_recv,
        x_send,
        x_recv,
        y_send,
        y_recv,
        core_own,
        core_send,
        core_recv,
        halo_send,
        halo_recv,
        coef_sem,
    ) = scratch
    smalls = [
        pltpu.make_async_copy(source, target, small_sem.at[i])
        for i, (source, target) in enumerate(
            (
                (load_in, load_ref),
                (send_in, send_ref),
                (frac_in, frac_ref),
                (diff_in, diff_ref),
                (drift_in, drift_ref),
                (loop_in, loop_ref),
                (rise_in, rise_ref),
            )
        )
    ]
    for copy in smalls:
        copy.start()
    me = lax.axis_index("phi")
    row = lax.axis_index("row")
    core = lax.rem(me, 2)
    x = lax.rem(me // 2, 2)
    y = me // 4
    sibling = me + 1 - 2 * core
    x_peer = me + 2 - 4 * x
    y_peer = me + 4 - 8 * y
    has_low = row > 0
    has_high = row < rows - 1
    lane = lax.broadcasted_iota(jnp.int32, (nz, LANES), 1)
    zrow = lax.broadcasted_iota(jnp.int32, (nz, LANES), 0)
    lane8 = lax.broadcasted_iota(jnp.int32, (8, LANES), 1)

    def own_copies(n, there):
        result = []
        for part, owns in enumerate((own_a, own_b)):
            z0 = pl.multiple_of(
                (1 - core if there else core) * (nz // 2) + (n % 2) * 16 + part * 8, 8
            )
            for t in range(tiles):
                source = fields_ref.at[n // 2, :, pl.ds(z0, 8), pl.ds(t * LANES, LANES)]
                target = owns[n].at[pl.ds((tiles * core + t) * radii, radii)]
                i = part * tiles + t
                if there:
                    result.append(
                        pltpu.make_async_remote_copy(
                            src_ref=source,
                            dst_ref=target,
                            send_sem=pair_send.at[n, i],
                            recv_sem=pair_recv.at[n, i],
                            device_id={"phi": sibling},
                            device_id_type=MESH,
                        )
                    )
                else:
                    result.append(pltpu.make_async_copy(source, target, own_sem.at[n, i]))
        return result

    for n in range(pairs):
        for copy in own_copies(n, False):
            copy.start()

    barrier = pltpu.get_barrier_semaphore()
    for peer in (sibling, x_peer, y_peer):
        pl.semaphore_signal(barrier, inc=1, device_id={"phi": peer}, device_id_type=MESH)

    @pl.when(has_low)
    def _():
        pl.semaphore_signal(barrier, inc=1, device_id={"row": row - 1}, device_id_type=MESH)

    @pl.when(has_high)
    def _():
        pl.semaphore_signal(barrier, inc=1, device_id={"row": row + 1}, device_id_type=MESH)

    inner = jnp.logical_and(has_low, has_high)

    @pl.when(inner)
    def _():
        pl.semaphore_wait(barrier, 5)

    @pl.when(jnp.logical_not(inner))
    def _():
        pl.semaphore_wait(barrier, 4)

    for n in range(pairs):
        for copy in own_copies(n, True):
            copy.start()

    def parts(n):
        result = []
        if n < pairs:
            result.append((0, EARLY))
        result.append((EARLY, slots if n > 0 else single))
        return result

    def message(axis, n, which):
        begin, end = parts(n)[which]
        source, target = (out_x, got_x) if axis == 0 else (out_y, got_y)
        sends, recvs = (x_send, x_recv) if axis == 0 else (y_send, y_recv)
        return pltpu.make_async_remote_copy(
            src_ref=source[n % 2].at[pl.ds(begin, end - begin)],
            dst_ref=target[n].at[pl.ds(begin, end - begin)],
            send_sem=sends.at[n, which],
            recv_sem=recvs.at[n, which],
            device_id={"phi": x_peer if axis == 0 else y_peer},
            device_id_type=MESH,
        )

    def placed(n):
        z0 = pl.multiple_of(core * (nz // 2) + (n % 2) * 16, 8)
        return state.at[n // 2, pl.ds(HALO, radii), pl.ds(z0, 16)]

    def core_keep(n):
        return pltpu.make_async_copy(stage[n % 2].at[core], placed(n), core_own.at[n])

    def core_give(n):
        return pltpu.make_async_remote_copy(
            src_ref=stage[n % 2].at[1 - core],
            dst_ref=placed(n),
            send_sem=core_send.at[n],
            recv_sem=core_recv.at[n],
            device_id={"phi": sibling},
            device_id_type=MESH,
        )

    def halo_copy(f, low):
        side = 0 if low else 1
        source = HALO if low else radii
        target = radii + HALO if low else 0
        return pltpu.make_async_remote_copy(
            src_ref=state.at[f, pl.ds(source, HALO)],
            dst_ref=state.at[f, pl.ds(target, HALO)],
            send_sem=halo_send.at[f, side],
            recv_sem=halo_recv.at[f, side],
            device_id={"row": row - 1 if low else row + 1},
            device_id_type=MESH,
        )

    def coef_copy(low):
        side = 0 if low else 1
        return pltpu.make_async_remote_copy(
            src_ref=coefs.at[pl.ds(HALO if low else radii, HALO)],
            dst_ref=coefs.at[pl.ds(radii + HALO if low else 0, HALO)],
            send_sem=coef_sem.at[side],
            recv_sem=coef_sem.at[2 + side],
            device_id={"row": row - 1 if low else row + 1},
            device_id_type=MESH,
        )

    for copy in smalls:
        copy.wait()

    def choose(code, first, second, third, last, rest):
        a = first[jnp.minimum(code, 2 * tiles * radii - 1)]
        b = second[jnp.minimum(jnp.maximum(code - 256, 0), last)]
        c = third[jnp.maximum(code - 512, rest)]
        return jnp.where(code < 256, a, jnp.where(code < 512, b, c))

    def pack(axis, n, which):
        begin, end = parts(n)[which]
        target = (out_x if axis == 0 else out_y)[n % 2]
        fresh = (own_a if axis == 0 else own_b)[min(n, pairs - 1)]
        older = (own_b if axis == 0 else own_a)[max(n - 1, 0)]
        passed = (got_y if axis == 0 else got_x)[max(n - 1, 0)]
        only = n == 0 or end <= EARLY

        def step(i, carry):
            for lag in range(group):
                slot = begin + i * group + lag
                code = send_ref[axis, slot]
                if only:
                    target[slot] = fresh[jnp.minimum(code, 2 * tiles * radii - 1)]
                else:
                    target[slot] = choose(
                        code, fresh, older, passed, 2 * tiles * radii - 1, 0
                    )
            return carry

        lax.fori_loop(0, (end - begin) // group, step, 0)
        message(axis, n, which).start()

    def arrived(n):
        for copy in own_copies(n, False):
            copy.wait()
        for copy in own_copies(n, True):
            copy.wait_recv()

    def shift(n):
        target = stage[n % 2]

        def shift_radius(r, carry):
            fine = load_ref[r, 32]
            turn = (LANES - fine) & (LANES - 1)
            inside = lane8 < jnp.full((8, LANES), LANES - fine, jnp.int32)
            weight = jnp.broadcast_to(coefs[HALO + r, 4:5, :], (8, LANES))
            keep = 1.0 - weight
            for part in range(2):
                owns = (own_a if part == 0 else own_b)[n]
                near = (got_x if part == 0 else got_y)[n]
                far = (got_y if part == 0 else got_x)[n + 1]
                cells = []
                for i in range(2 * tiles + 3):
                    code = load_ref[r, 16 * part + i]
                    cells.append(
                        pltpu.roll(choose(code, owns, near, far, single - 1, EARLY), turn, 1)
                    )
                cells = [
                    jnp.where(inside, cells[i], cells[i + 1]) for i in range(2 * tiles + 2)
                ]
                turned = [pltpu.roll(c, 1, 1) for c in cells]
                moved = []
                for i in range(2 * tiles + 2):
                    before = turned[i]
                    if i > 0:
                        before = jnp.where(lane8 == 0, turned[i - 1], turned[i])
                    moved.append(keep * cells[i] + weight * before)
                z0 = 8 * part
                for half in range(2):
                    base = half * tiles
                    for t in range(tiles):
                        target[half, r, z0 : z0 + 8, t * LANES : (t + 1) * LANES] = moved[
                            base + t + 1
                        ]
                    target[half, r, z0 : z0 + 8, width : width + LANES] = jnp.where(
                        lane8 < LANES // 2, moved[base + tiles + 1], moved[base]
                    )
            return carry

        lax.fori_loop(0, radii, shift_radius, 0)
        core_keep(n).start()
        core_give(n).start()

    def blend(cur, prev_tile, next_tile, up, low, where_r, height, height2):
        k_up = coefs[where_r, 0:1, :]
        k_low = coefs[where_r, 1:2, :]
        k_loop = coefs[where_r, 2:3, :]
        k_mid = coefs[where_r, 3:4, :]
        west = jnp.where(lane == 0, pltpu.roll(prev_tile, 1, 1), pltpu.roll(cur, 1, 1))
        east = jnp.where(
            lane == LANES - 1,
            pltpu.roll(next_tile, LANES - 1, 1),
            pltpu.roll(cur, LANES - 1, 1),
        )
        below = jnp.where(zrow == 0, 0.0, pltpu.roll(cur, 1, 0))
        above = jnp.where(zrow == nz - 1, 0.0, pltpu.roll(cur, nz - 1, 0))
        total = (k_mid - height2) * cur + k_up * up + k_low * low
        return total + k_loop * (east + west) + height * (above + below)

    def first_substep(f, which):
        begin, end = ((1, radii + 3), (HALO + 1, radii + 1), (0, 2 * HALO))[which]

        def first(i, carry):
            if which == 2:
                i = jnp.where(i < HALO, i + 1, i + radii - 1)
            height = height_ref[...]
            height2 = height + height

            def tile(r, t):
                return state[f, r, :, pl.ds(t * LANES, LANES)]

            for t in range(tiles + 1):
                mid[i - 1, :, pl.ds(t * LANES, LANES)] = blend(
                    tile(i, t),
                    tile(i, (t + tiles) % (tiles + 1)),
                    tile(i, (t + 1) % (tiles + 1)),
                    tile(i + 1, t),
                    tile(i - 1, t),
                    i,
                    height,
                    height2,
                )
            return carry

        lax.fori_loop(begin, end, first, 0)

    def substeps(f):
        @pl.when(has_low)
        def _():
            halo_copy(f, False).wait_recv()

        @pl.when(has_high)
        def _():
            halo_copy(f, True).wait_recv()

        first_substep(f, 2 if f == fields - 1 else 0)

        @pl.when(jnp.logical_not(has_low))
        def _():
            mid[0] = jnp.zeros(mid.shape[1:], jnp.float32)

        @pl.when(jnp.logical_not(has_high))
        def _():
            mid[radii + 1] = jnp.zeros(mid.shape[1:], jnp.float32)

        def second(i, carry):
            height = height_ref[...]
            height2 = height + height

            def tile(r, t):
                return mid[r, :, pl.ds(t * LANES, LANES)]

            for t in range(tiles):
                out_ref[f, i - 1, :, pl.ds(t * LANES, LANES)] = blend(
                    tile(i, t),
                    tile(i, (t + tiles) % (tiles + 1)),
                    tile(i, (t + 1) % (tiles + 1)),
                    tile(i + 1, t),
                    tile(i - 1, t),
                    i + 1,
                    height,
                    height2,
                )
            return carry

        lax.fori_loop(1, radii + 1, second, 0)

    settled = set()

    def settle(n):
        if n not in settled:
            settled.add(n)
            core_keep(n).wait()

    arrived(0)
    for which in range(2):
        for axis in range(2):
            pack(axis, 0, which)

    def fill_coefs(i, carry):
        diff = jnp.full((1, LANES), diff_ref[i], jnp.float32)
        drift = jnp.full((1, LANES), drift_ref[i], jnp.float32)
        loop = jnp.full((1, LANES), loop_ref[i], jnp.float32)
        coefs[HALO + i, 0:1, :] = diff + drift
        coefs[HALO + i, 1:2, :] = diff - drift
        coefs[HALO + i, 2:3, :] = loop
        coefs[HALO + i, 3:4, :] = 1.0 - 2.0 * (diff + loop)
        coefs[HALO + i, 4:5, :] = jnp.full((1, LANES), frac_ref[i], jnp.float32)
        coefs[HALO + i, 5:8, :] = jnp.zeros((3, LANES), jnp.float32)
        return carry

    lax.fori_loop(0, radii, fill_coefs, 0)

    def fill_height(z, carry):
        height_ref[pl.ds(z, 1), :] = jnp.full((1, LANES), rise_ref[z], jnp.float32)
        return carry

    lax.fori_loop(0, nz, fill_height, 0)

    @pl.when(has_low)
    def _():
        coef_copy(True).start()

    @pl.when(has_high)
    def _():
        coef_copy(False).start()

    @pl.when(jnp.logical_not(has_low))
    def _():
        state[:, 0:HALO] = jnp.zeros((fields, HALO) + state.shape[2:], jnp.float32)
        coefs[0:HALO] = jnp.zeros((HALO,) + coefs.shape[1:], jnp.float32)

    @pl.when(jnp.logical_not(has_high))
    def _():
        state[:, radii + HALO :] = jnp.zeros((fields, HALO) + state.shape[2:], jnp.float32)
        coefs[radii + HALO :] = jnp.zeros((HALO,) + coefs.shape[1:], jnp.float32)

    arrived(1)
    for axis in range(2):
        pack(axis, 1, 0)

    @pl.when(has_low)
    def _():
        coef_copy(False).wait_recv()

    @pl.when(has_high)
    def _():
        coef_copy(True).wait_recv()

    for n in range(1, pairs + 3):
        if n <= pairs + 1:
            for axis in range(2):
                for which in range(len(parts(n - 1))):
                    message(axis, n - 1, which).wait_recv()
        if n <= pairs:
            last = len(parts(n)) - 1
            if n == pairs:
                for axis in range(2):
                    for which in range(2):
                        message(axis, n - 2, which).wait_send()
            for axis in range(2):
                pack(axis, n, last)
        if n + 1 < pairs:
            arrived(n + 1)
            for axis in range(2):
                for which in range(2):
                    message(axis, n - 1, which).wait_send()
                pack(axis, n + 1, 0)
        if 2 <= n <= pairs + 1:
            if n >= 4:
                settle(n - 4)
                core_give(n - 4).wait_send()
            shift(n - 2)
        f = (n - 4) // 2
        if n >= 4 and n % 2 == 0 and f < fields:
            for pair in (2 * f, 2 * f + 1):
                settle(pair)
                core_give(pair).wait_recv()

            @pl.when(has_low)
            def _(f=f):
                halo_copy(f, True).start()

            @pl.when(has_high)
            def _(f=f):
                halo_copy(f, False).start()

            if f == fields - 1:
                first_substep(f, 1)
            if n >= pairs:
                substeps(f)

        f = (n - 5) // 2
        if n >= 5 and n % 2 == 1 and n < pairs:
            substeps(f)

    for axis in range(2):
        for n in (pairs - 1, pairs):
            for which in range(len(parts(n))):
                message(axis, n, which).wait_send()
    for n in range(pairs):
        for copy in own_copies(n, True):
            copy.wait_send()
    for n in (pairs - 2, pairs - 1):
        core_give(n).wait_send()
    for f in range(fields):

        @pl.when(has_low)
        def _(f=f):
            halo_copy(f, True).wait_send()

        @pl.when(has_high)
        def _(f=f):
            halo_copy(f, False).wait_send()

    @pl.when(has_low)
    def _():
        coef_copy(True).wait_send()

    @pl.when(has_high)
    def _():
        coef_copy(False).wait_send()


def routed(rows, slots, which, load, send, fraction, radial_diff, radial_drift, loop_diff, height_diff, fields):
    count, radii, nz, width = fields.shape
    tiles = width // LANES
    pairs = 2 * count
    full = radii + 2 * HALO
    wide = width + LANES
    f32 = jnp.float32
    dma = pltpu.SemaphoreType.DMA
    scratch = [pltpu.VMEM((2 * tiles * radii, 8, LANES), f32)] * (2 * pairs)
    scratch += [pltpu.VMEM((slots, 8, LANES), f32)] * (2 * pairs + 2 + 4)
    scratch += [pltpu.VMEM((2, radii, 16, wide), f32)] * 2
    scratch += [
        pltpu.VMEM((count, full, nz, wide), f32),
        pltpu.VMEM((full - 2, nz, wide), f32),
        pltpu.VMEM((full, 8, LANES), f32),
        pltpu.VMEM((nz, LANES), f32),
        pltpu.SMEM(load.shape, jnp.int32),
        pltpu.SMEM(send.shape, jnp.int32),
        pltpu.SMEM((radii,), f32),
        pltpu.SMEM((radii,), f32),
        pltpu.SMEM((radii,), f32),
        pltpu.SMEM((radii,), f32),
        pltpu.SMEM((nz,), f32),
        dma((7,)),
        dma((pairs, 2 * tiles)),
        dma((pairs, 2 * tiles)),
        dma((pairs, 2 * tiles)),
        dma((pairs + 1, 2)),
        dma((pairs + 1, 2)),
        dma((pairs + 1, 2)),
        dma((pairs + 1, 2)),
        dma((pairs,)),
        dma((pairs,)),
        dma((pairs,)),
        dma((count, 2)),
        dma((count, 2)),
        dma((4,)),
    ]
    hbm = pl.BlockSpec(memory_space=pltpu.HBM)
    return pl.pallas_call(
        functools.partial(routed_kernel, rows, slots),
        out_shape=pltpu.VMEM(fields.shape, f32),
        in_specs=[hbm] * 8,
        out_specs=pl.BlockSpec(memory_space=pltpu.VMEM),
        scratch_shapes=scratch,
        compiler_params=pltpu.CompilerParams(
            collective_id=2 + which, has_side_effects=True, vmem_limit_bytes=56557568
        ),
    )(load, send, fraction, radial_diff, radial_drift, loop_diff, height_diff, fields)


def plan(rows, offsets):
    radii = offsets.shape[0]
    i32 = jnp.int32
    dma = pltpu.SemaphoreType.DMA
    vmem = pl.BlockSpec(memory_space=pltpu.VMEM)
    smem = pl.BlockSpec(memory_space=pltpu.SMEM)
    return pl.pallas_call(
        functools.partial(plan_kernel, rows, LEVELS),
        out_shape=(
            jax.ShapeDtypeStruct((radii, LANES), i32),
            jax.ShapeDtypeStruct((8, 2 * LANES), i32),
            jax.ShapeDtypeStruct((1,), i32),
        ),
        in_specs=[smem],
        out_specs=(vmem, vmem, smem),
        scratch_shapes=[
            pltpu.VMEM((8, LANES), jnp.float32),
            pltpu.VMEM((rows, 8, LANES), jnp.float32),
            dma((rows,)),
            dma((rows,)),
        ],
        compiler_params=pltpu.CompilerParams(collective_id=1, has_side_effects=True),
    )(offsets)


def adaptive(n, rows, fields, offsets, fraction, radial_diff, radial_drift, loop_diff, height_diff):
    if (n, fields.shape[1:]) != (ROUTED, (16, 64, 4 * LANES)):
        return local(
            n, rows, fields, offsets, fraction, radial_diff, radial_drift, loop_diff, height_diff
        )
    load, send, level = plan(rows, offsets)

    def through(which):
        return lambda load, send, offsets, *rest: routed(rows, LEVELS[which], which, load, send, *rest)

    def whole(load, send, offsets, fraction, radial_diff, radial_drift, loop_diff, height_diff, fields):
        return local(
            n, rows, fields, offsets, fraction, radial_diff, radial_drift, loop_diff, height_diff
        )

    branches = [through(which) for which in range(len(LEVELS))] + [whole]
    return lax.switch(
        level[0], branches, load, send, offsets, fraction, radial_diff, radial_drift, loop_diff,
        height_diff, fields,
    )


def solution(mesh):
    placed = (P(None, "row", None, "phi"), P("row"), P("row"), P("row"), P("row"), P("row"), P())
    body = functools.partial(adaptive, mesh.shape["phi"], mesh.shape["row"])
    return jax.shard_map(
        body, mesh=mesh, in_specs=placed, out_specs=P(None, "row", None, "phi"), check_vma=False
    )
```
